32 devices in a mesh: rep: 2 (over x), node: 8 (over z, y), local: 2 (over core).
Axes of the slice: x: 2, y: 2, z: 4, core: 2. Of those that a mesh axis runs over, the one named last changes fastest.
Arguments:
- tokens: bfloat16 [2048, 7168], P(('rep', 'node', 'local')), parts along dimension 0, may hold values from -6 to 6
- gate_ids: int32 [2048, 4], P(('rep', 'node', 'local')), parts along dimension 0, may hold values from 0 to 7, all different within a row; in each aligned block of 64 rows (0 to 63, 64 to 127, ...) at most 64 rows name the same one
- gate_values: bfloat16 [2048, 4], P(('rep', 'node', 'local')), parts along dimension 0, may hold values from 0.049804688 to 1
- w_gate: bfloat16 [8, 7168, 1024], P('node', None, 'local'), may hold values from -0.0625 to 0.0625
- w_up: bfloat16 [8, 7168, 1024], P('node', None, 'local'), may hold values from -0.0625 to 0.0625
- w_down: bfloat16 [8, 1024, 7168], P('node', 'local'), may hold values from -0.1875 to 0.1875
Outputs:
- mixed: bfloat16 [2048, 7168], P(('rep', 'node', 'local')), parts along dimension 0
The draws below stay inside these ranges and needn't reach their ends.
There are 2 independent parts, one for each index of `rep`. The reference program is written for one: setup_inputs(seed, part) draws one part's arguments, and reference() takes and returns one part's arrays. A program takes and returns all parts, laid end to end along the dimension named above; an argument that names none is the same for every part. Nothing has to cross between parts.
Inputs may be any that keep to these rules, and one draw needn't show every extreme that they name: `gate_ids`: each row names 4 different experts. Within the rows of one device, no expert is named by more than 64 rows, and in every draw some expert is named by exactly 64 rows of some device.
All inputs are finite; a program needn't handle non-finite values.
Results may differ from the reference program's by a relative error of at most 0.0065.
Values may be sent and summed in bfloat16 or wider, within the bound.
A program may use at most 128 MiB of HBM per device.

```python
import math
import jax
import jax.numpy as jnp
import numpy as np
from jax import lax

D = 7168
HID = 1024
TOPK = 4
TOK_DEV = 64
EXPERTS = 8
CAP = 64
TOKENS = 1024
N_NODE = 8
N_LOCAL = 2


def block_levels(own_key, dims, shards, least, high):
    level, own = 1.0, jax.random.fold_in(own_key, 6)
    for axis_at, shards_of in shards:
        steps = jnp.exp(jax.random.uniform(jax.random.fold_in(own, axis_at), (shards_of,), jnp.float32, least / len(shards), high / len(shards)))
        level = level * jnp.repeat(steps, dims[axis_at] // shards_of).reshape([-1 if axis == axis_at else 1 for axis in range(len(dims))])
    return level


def shared_out(own_key, own, number, rows, amount, top, limit, lean):
    order = jax.random.permutation(own_key, amount)
    crowded, common = shares(amount, rows * top, limit, lean, True), shares(amount, rows * top, limit, lean, False)
    places = jnp.arange(amount)

    def named(tallies, rotation):
        used = int((tallies > 0).sum())
        fixed = max(1, used // 4)
        moved = fixed + (places - fixed + rotation * (used - fixed)) % max(1, amount - fixed)
        return jnp.zeros((amount,), jnp.int32).at[order[jnp.where(places < fixed, places, moved)]].set(jnp.asarray(tallies, jnp.int32))

    tallies = jnp.where(number % 4 == 0, named(crowded, number // 4), named(common, number - number // 4 - 1))
    mixed = jax.random.permutation(jax.random.fold_in(own, 3), amount)
    source_of, receiver = mixed[0:amount // 2 * 2:2], mixed[1:amount // 2 * 2:2]
    slack = jnp.minimum(tallies[source_of] - 1, limit - tallies[receiver]) // 2
    slack = jnp.where((source_of == order[0]) | (receiver == order[0]) | (tallies[receiver] == 0), 0, jnp.maximum(slack, 0))
    moved = jax.random.randint(jax.random.fold_in(own, 4), (amount // 2,), 0, 1 << 20) % (slack + 1)
    tallies = tallies.at[source_of].add(-moved).at[receiver].add(moved)
    members = jnp.searchsorted(jnp.cumsum(tallies), jnp.arange(rows * top), side="right").astype(jnp.int32)
    listing = members.reshape(top, rows).T
    listing = listing[jax.random.permutation(jax.random.fold_in(own, 1), rows)]
    rotation = jax.random.randint(jax.random.fold_in(own, 2), (rows, 1), 0, top)
    return jnp.take_along_axis(listing, (jnp.arange(top)[None, :] + rotation) % top, axis=1)


def shares(number_of, total, reach, slope, full):
    weights = [(1 << 20) // math.isqrt(grade ** slope) + 1 for grade in range(1, number_of + 1)]
    largest = reach if full else min(reach, max(-(-total // number_of), total * weights[0] // sum(weights)))
    least = 1 if total - largest >= number_of - 1 else 0
    given, surplus = [largest] + [least] * (number_of - 1), total - largest - least * (number_of - 1)
    while surplus > 0:
        movable = [i for i in range(1, number_of) if given[i] < largest] or [i for i in range(1, number_of) if given[i] < reach]
        pool, left = sum([weights[i] for i in movable]), surplus
        for i in movable:
            addition = min(reach - given[i], max(1, left * weights[i] // pool), surplus)
            given[i] = given[i] + addition
            surplus = surplus - addition
    return np.array(given)


def normal_values(own_key, shape, scale, reach, shards=(), kind=jnp.bfloat16):
    factor_of = block_levels(own_key, shape, shards, -0.22, 0.18) if shards else 1.0
    array = jax.random.normal(own_key, shape, jnp.float32) * scale * factor_of
    return jnp.minimum(jnp.maximum(array, -reach), reach).astype(kind)


def setup_inputs(seed: int = 0, part: int = 0) -> dict:
    splits = jax.random.split(jax.random.key(seed), 7)
    part_splits = jax.random.split(jax.random.fold_in(splits[6], part), 7)
    tokens = normal_values(part_splits[0], (TOKENS, D), 1.0, 6.0, ((0, 16),))
    gate_ids_keys = jax.random.split(jax.random.fold_in(part_splits[1], 1), TOKENS // TOK_DEV)
    gate_ids_turns = jax.random.permutation(jax.random.fold_in(part_splits[1], 3), TOKENS // TOK_DEV)
    gate_ids = jax.vmap(lambda own, number: shared_out(jax.random.fold_in(part_splits[1], 2), own, number, TOK_DEV, EXPERTS, TOPK, CAP, 2))(gate_ids_keys, gate_ids_turns).reshape((TOKENS, TOPK))
    gate_values = jnp.clip(jnp.exp(math.log(1.0) - 2.9996462 * jax.random.uniform(part_splits[2], (TOKENS, TOPK), jnp.float32) ** block_levels(part_splits[2], (TOKENS, TOPK), ((0, 16),), -0.2, 0.2)), 0.049804688, 1.0).astype(jnp.bfloat16)
    w_gate = normal_values(splits[3], (EXPERTS, D, HID), D ** -0.5, 0.0625, ((0, 8), (2, 2)))
    w_up = normal_values(splits[4], (EXPERTS, D, HID), D ** -0.5, 0.0625, ((0, 8), (2, 2)))
    w_down = normal_values(splits[5], (EXPERTS, HID, D), HID ** -0.5, 0.1875, ((0, 8), (1, 2)))
    return {"tokens": tokens, "gate_ids": gate_ids, "gate_values": gate_values, "w_gate": w_gate, "w_up": w_up, "w_down": w_down}


def slot_tables(gate_ids, gate_values):
    flat_ids = gate_ids.reshape(-1).astype(jnp.int32)
    expert_row = jnp.arange(EXPERTS, dtype=jnp.int32)
    onehot = (flat_ids[:, None] == expert_row[None, :]).astype(jnp.int32)
    earlier = jnp.cumsum(onehot, axis=0) - onehot
    within = jnp.sum(earlier * onehot, axis=1).astype(jnp.int32)
    slot = (flat_ids * CAP + within).reshape(TOK_DEV, TOPK)
    slot_row = jnp.arange(EXPERTS * CAP, dtype=jnp.int32)
    matches = slot[:, :, None] == slot_row[None, None, :]
    select = jnp.any(matches, axis=1).astype(jnp.bfloat16)
    combine_table = jnp.sum(jnp.where(matches, gate_values.astype(jnp.float32)[:, :, None], jnp.float32(0.0)), axis=1).astype(jnp.bfloat16)
    return select, combine_table


def expert_rows(args):
    rows, gate_mat, up_mat, down_mat = args
    gate_act = jnp.dot(rows, gate_mat, preferred_element_type=jnp.float32)
    up_act = jnp.dot(rows, up_mat, preferred_element_type=jnp.float32)
    hidden = (jax.nn.silu(gate_act) * up_act).astype(jnp.bfloat16)
    group = HID // N_LOCAL
    summed = jnp.zeros((rows.shape[0], D), jnp.float32)
    for part_index in range(N_LOCAL):
        piece = jnp.dot(hidden[:, part_index * group:(part_index + 1) * group], down_mat[part_index * group:(part_index + 1) * group], preferred_element_type=jnp.float32).astype(jnp.bfloat16)
        piece = lax.optimization_barrier(piece)
        summed = summed + piece.astype(jnp.float32)
    return summed.astype(jnp.bfloat16)


def reference(tokens, gate_ids, gate_values, w_gate, w_up, w_down):
    devices = N_NODE * N_LOCAL
    token_blocks = tokens.reshape(devices, TOK_DEV, D)
    select, combine_table = jax.vmap(slot_tables)(gate_ids.reshape(devices, TOK_DEV, TOPK), gate_values.reshape(devices, TOK_DEV, TOPK))
    dispatched = jnp.einsum("nts,ntd->nsd", select.astype(jnp.float32), token_blocks.astype(jnp.float32), precision=lax.Precision.HIGHEST).astype(jnp.bfloat16)
    by_expert = dispatched.reshape(devices, EXPERTS, CAP, D).transpose(1, 0, 2, 3).reshape(EXPERTS, devices * CAP, D)
    expert_out = lax.map(expert_rows, (by_expert, w_gate, w_up, w_down))
    back = expert_out.reshape(EXPERTS, devices, CAP, D).transpose(1, 0, 2, 3).reshape(devices, EXPERTS * CAP, D)
    mixed = jnp.einsum("nts,nsd->ntd", combine_table.astype(jnp.float32), back.astype(jnp.float32), precision=lax.Precision.HIGHEST)
    return mixed.astype(jnp.bfloat16).reshape(TOKENS, D)
```

```python
import jax
import jax.numpy as jnp
from jax import lax
from jax.sharding import PartitionSpec as P


def per_device(tokens, gate_ids, gate_values, w_gate, w_up, w_down):
    node_count = lax.axis_size("node")
    expert_row = jnp.arange(node_count, dtype=jnp.int32)
    weight = jnp.sum(
        jnp.where(
            gate_ids[:, :, None] == expert_row[None, None, :],
            gate_values.astype(jnp.float32)[:, :, None],
            jnp.float32(0.0),
        ),
        axis=1,
    ).astype(jnp.bfloat16)
    every = ("node", "local")
    weights = lax.all_gather(weight, every, axis=0, tiled=True)
    rows = lax.all_gather(tokens, every, axis=0, tiled=True)
    mine = (expert_row == lax.axis_index("node"))[None, :]
    scale = jnp.sum(jnp.where(mine, weights.astype(jnp.float32), 0.0), axis=1, keepdims=True)
    gate_act = jnp.dot(rows, w_gate[0], preferred_element_type=jnp.float32)
    up_act = jnp.dot(rows, w_up[0], preferred_element_type=jnp.float32)
    hidden = (jax.nn.silu(gate_act) * up_act).astype(jnp.bfloat16)
    partial_value = jnp.dot(hidden, w_down[0], preferred_element_type=jnp.float32) * scale
    return lax.psum_scatter(
        partial_value.astype(jnp.bfloat16), every, scatter_dimension=0, tiled=True
    )


def solution(mesh):
    return jax.shard_map(
        per_device,
        mesh=mesh,
        in_specs=(
            P(("rep", "node", "local"), None),
            P(("rep", "node", "local"), None),
            P(("rep", "node", "local"), None),
            P("node", None, "local"),
            P("node", None, "local"),
            P("node", "local", None),
        ),
        out_specs=P(("rep", "node", "local"), None),
        check_vma=False,
    )
```

```python
import functools

import jax
import jax.numpy as jnp
from jax import lax
from jax.experimental import pallas as pl
from jax.experimental.pallas import tpu as pltpu
from jax.sharding import PartitionSpec as P

MESH = pl.DeviceIdType.MESH
LANES = 128
VMEM_LIMIT = 67_000_000


def chunk_of(size, most=1024):
    chunk = most
    while size % chunk:
        chunk -= LANES
    return chunk


def expert_weights(gate_ids, gate_values, columns):
    expert_row = jnp.arange(columns, dtype=jnp.int32)
    return jnp.sum(
        jnp.where(
            gate_ids[:, :, None] == expert_row[None, None, :],
            gate_values.astype(jnp.float32)[:, :, None],
            jnp.float32(0.0),
        ),
        axis=1,
    ).astype(jnp.bfloat16)


def ring_kernel(
    n, block, wg_hbm, wu_hbm, wd_hbm, out,
    x, wg, wu, wd, ring_in, pin, pout, acc, own, gate_acc, up_acc,
    weight_sem, own_sem, ag_send, ag_recv, pa_send, pa_recv,
    pp_send, pp_recv, rs_send, rs_recv,
):
    tok, wide = block.shape
    width = wg.shape[0]
    half = tok // 2
    depth = n // 2
    node = lax.axis_index("node")
    partner = 1 - lax.axis_index("local")
    row, column = node // 2, node % 2
    place = row * (1 - column) + (n - 1 - row) * column

    def node_at(position):
        side = position // depth
        level = position * (1 - side) + (n - 1 - position) * side
        return 2 * level + side

    to = (node_at((place + 1) % n), node_at((place + n - 1) % n))

    loads = [
        pltpu.make_async_copy(src, dst, weight_sem.at[k])
        for k, (src, dst) in enumerate(((wg_hbm, wg), (wu_hbm, wu), (wd_hbm, wd)))
    ]
    keep = pltpu.make_async_copy(block, x.at[0, pl.ds(0, tok)], own_sem.at[0])

    barrier = pltpu.get_barrier_semaphore()
    for target in ({"node": to[0]}, {"node": to[1]}, {"local": partner}):
        pl.semaphore_signal(barrier, inc=1, device_id=target, device_id_type=MESH)
    pl.semaphore_wait(barrier, 3)

    def rows_of(d):
        return pl.ds(d * half, half)

    def ag(step, d, src):
        return pltpu.make_async_remote_copy(
            src_ref=src, dst_ref=x.at[step, rows_of(d)],
            send_sem=ag_send.at[step, d], recv_sem=ag_recv.at[step, d],
            device_id={"node": to[d]}, device_id_type=MESH,
        )

    def pa(step, src):
        return pltpu.make_async_remote_copy(
            src_ref=src, dst_ref=x.at[step, pl.ds(tok, tok)],
            send_sem=pa_send.at[step], recv_sem=pa_recv.at[step],
            device_id={"local": partner}, device_id_type=MESH,
        )

    def pp(step, slot):
        return pltpu.make_async_remote_copy(
            src_ref=pout.at[slot], dst_ref=pin.at[step],
            send_sem=pp_send.at[slot], recv_sem=pp_recv.at[step],
            device_id={"local": partner}, device_id_type=MESH,
        )

    def rs(i, d, slot):
        return pltpu.make_async_remote_copy(
            src_ref=acc.at[slot, rows_of(d)], dst_ref=ring_in.at[i - 1, rows_of(d)],
            send_sem=rs_send.at[slot, d], recv_sem=rs_recv.at[i - 1, d],
            device_id={"node": to[d]}, device_id_type=MESH,
        )

    ag(1, 0, block.at[rows_of(0)]).start()
    ag(1, 1, block.at[rows_of(1)]).start()
    for load in loads:
        load.start()
    pa(0, block).start()
    keep.start()

    kc = chunk_of(width)

    def compute(step, slot):
        gate_acc[...] = jnp.zeros_like(gate_acc)
        up_acc[...] = jnp.zeros_like(up_acc)

        @pl.loop(0, width // kc)
        def _(k):
            cols = pl.ds(pl.multiple_of(k * kc, LANES), kc)
            rows = x[step, :, cols]
            gate_acc[...] += jnp.dot(rows, wg[cols, :], preferred_element_type=jnp.float32)
            up_acc[...] += jnp.dot(rows, wu[cols, :], preferred_element_type=jnp.float32)

        gate = gate_acc[...]
        hidden = (gate / (1.0 + jnp.exp(-gate)) * up_acc[...]).astype(jnp.bfloat16)
        table = x[step, :, pl.ds(width, LANES)].astype(jnp.float32)
        lane = lax.broadcasted_iota(jnp.int32, table.shape, 1)
        scale = jnp.sum(jnp.where(lane == node, table, 0.0), axis=1, keepdims=True)

        @pl.loop(0, width // kc)
        def _(k):
            cols = pl.ds(pl.multiple_of(k * kc, LANES), kc)
            value = jnp.dot(hidden, wd[:, cols], preferred_element_type=jnp.float32) * scale
            own[:, cols] = value[:tok]
            pout[slot, :, cols] = value[tok:].astype(jnp.bfloat16)

    def combine(step, i, d, dst, first):
        @pl.loop(0, width // kc)
        def _(k):
            cols = pl.ds(pl.multiple_of(k * kc, LANES), kc)
            value = own[rows_of(d), cols] + pin[step, rows_of(d), cols].astype(jnp.float32)
            if not first:
                value += ring_in[i - 2, rows_of(d), cols].astype(jnp.float32)
            dst[rows_of(d), cols] = value.astype(jnp.bfloat16)

    def gather_step(i, forward):
        for d in range(2):
            ag(i, d, block.at[rows_of(d)]).wait_recv()
            if forward:
                ag(i + 1, d, x.at[i, rows_of(d)]).start()
        pa(i, x.at[i, pl.ds(0, tok)]).start()
        pa(i, x.at[i, pl.ds(0, tok)]).wait_recv()

    def reduce_step(i, first):
        slot = i % 2
        pp(i, slot).start()
        pp(i, slot).wait_recv()
        for d in range(2):
            if not first:
                rs(i - 1, d, slot).wait_recv()
            combine(i, i, d, acc.at[slot], first)
            rs(i, d, slot).start()

    def free_slot(i):
        slot = i % 2

        @pl.when(i >= 3)
        def _():
            pp(i, slot).wait_send()
            for d in range(2):
                rs(i, d, slot).wait_send()

    gather_step(1, True)
    for load in loads:
        load.wait()
    compute(1, 1)
    reduce_step(1, True)

    @pl.loop(2, n - 1)
    def _(i):
        gather_step(i, True)
        free_slot(i)
        compute(i, i % 2)
        reduce_step(i, False)

    gather_step(n - 1, False)
    free_slot(n - 1)
    compute(n - 1, (n - 1) % 2)
    reduce_step(n - 1, False)

    last = n % 2
    keep.wait()
    pa(0, block).wait_recv()
    pp(0, last).wait_send()
    compute(0, last)
    pp(0, last).start()
    pp(0, last).wait_recv()
    for d in range(2):
        rs(n - 1, d, last).wait_recv()
        combine(0, n, d, out, False)
    for d in range(2):
        for slot in range(2):
            rs(1, d, slot).wait_send()

        @pl.loop(1, n)
        def _(i):
            ag(i, d, block.at[rows_of(d)]).wait_send()

    for slot in range(2):
        pp(0, slot).wait_send()

    @pl.loop(0, n)
    def _(i):
        pa(i, block).wait_send()


def by_ring(n, tokens, gate_ids, gate_values, w_gate, w_up, w_down):
    tok, width = tokens.shape
    hid = w_gate.shape[2]
    half_type = jnp.bfloat16
    block = jnp.concatenate([tokens, expert_weights(gate_ids, gate_values, LANES)], axis=1)
    anywhere = pl.BlockSpec(memory_space=pl.ANY)
    dma = pltpu.SemaphoreType.DMA
    return pl.pallas_call(
        functools.partial(ring_kernel, n),
        out_shape=jax.ShapeDtypeStruct((tok, width), half_type),
        in_specs=[anywhere] * 4,
        out_specs=pl.BlockSpec(memory_space=pltpu.VMEM),
        scratch_shapes=[
            pltpu.VMEM((n, 2 * tok, width + LANES), half_type),
            pltpu.VMEM((width, hid), half_type),
            pltpu.VMEM((width, hid), half_type),
            pltpu.VMEM((hid, width), half_type),
            pltpu.VMEM((n - 1, tok, width), half_type),
            pltpu.VMEM((n, tok, width), half_type),
            pltpu.VMEM((2, tok, width), half_type),
            pltpu.VMEM((2, tok, width), half_type),
            pltpu.VMEM((tok, width), jnp.float32),
            pltpu.VMEM((2 * tok, hid), jnp.float32),
            pltpu.VMEM((2 * tok, hid), jnp.float32),
            dma((3,)), dma((1,)), dma((n, 2)), dma((n, 2)), dma((n,)), dma((n,)),
            dma((2,)), dma((n,)), dma((2, 2)), dma((n - 1, 2)),
        ],
        compiler_params=pltpu.CompilerParams(
            collective_id=0, has_side_effects=True, vmem_limit_bytes=VMEM_LIMIT
        ),
    )(block, w_gate[0], w_up[0], w_down[0])


def by_collectives(tokens, gate_ids, gate_values, w_gate, w_up, w_down):
    n = lax.axis_size("node")
    every = ("node", "local")
    weights = lax.all_gather(expert_weights(gate_ids, gate_values, n), every, axis=0, tiled=True)
    rows = lax.all_gather(tokens, every, axis=0, tiled=True)
    mine = (jnp.arange(n, dtype=jnp.int32) == lax.axis_index("node"))[None, :]
    scale = jnp.sum(jnp.where(mine, weights.astype(jnp.float32), 0.0), axis=1, keepdims=True)
    gate_act = jnp.dot(rows, w_gate[0], preferred_element_type=jnp.float32)
    up_act = jnp.dot(rows, w_up[0], preferred_element_type=jnp.float32)
    hidden = (jax.nn.silu(gate_act) * up_act).astype(jnp.bfloat16)
    partial_value = jnp.dot(hidden, w_down[0], preferred_element_type=jnp.float32) * scale
    return lax.psum_scatter(
        partial_value.astype(jnp.bfloat16), every, scatter_dimension=0, tiled=True
    )


def ring_fits(n, tok, width, hid):
    rows = n * 2 * tok + (n - 1) * tok + n * tok + 7 * tok
    return 2 * width * (rows + 3 * hid) + 8 * 2 * tok * hid + 2**21 < VMEM_LIMIT


def per_device(tokens, gate_ids, gate_values, w_gate, w_up, w_down):
    n = lax.axis_size("node")
    fits = ring_fits(n, tokens.shape[0], tokens.shape[1], w_gate.shape[2])
    if n % 2 == 0 and n >= 4 and lax.axis_size("local") == 2 and n <= LANES and fits:
        return by_ring(n, tokens, gate_ids, gate_values, w_gate, w_up, w_down)
    return by_collectives(tokens, gate_ids, gate_values, w_gate, w_up, w_down)


def solution(mesh):
    return jax.shard_map(
        per_device,
        mesh=mesh,
        in_specs=(
            P(("rep", "node", "local"), None),
            P(("rep", "node", "local"), None),
            P(("rep", "node", "local"), None),
            P("node", None, "local"),
            P("node", None, "local"),
            P("node", "local", None),
        ),
        out_specs=P(("rep", "node", "local"), None),
        check_vma=False,
    )
```

```python
import functools

import jax
import jax.numpy as jnp
from jax import lax
from jax.experimental import pallas as pl
from jax.experimental.pallas import tpu as pltpu
from jax.sharding import PartitionSpec as P

MESH = pl.DeviceIdType.MESH
LANES = 128
VMEM_LIMIT = 67_000_000


def chunk_of(size, most=1024):
    chunk = most
    while size % chunk:
        chunk -= LANES
    return chunk


def expert_weights(gate_ids, gate_values, columns):
    expert_row = jnp.arange(columns, dtype=jnp.int32)
    return jnp.sum(
        jnp.where(
            gate_ids[:, :, None] == expert_row[None, None, :],
            gate_values.astype(jnp.float32)[:, :, None],
            jnp.float32(0.0),
        ),
        axis=1,
    ).astype(jnp.bfloat16)


def ring_kernel(
    n, tokens, ids, values, wg_hbm, wu_hbm, wd_hbm, out,
    x, wg, wu, wd, ring_in, pin, pout, acc, own, gate_acc, up_acc,
    weight_sem, own_sem, ag_send, ag_recv, pa_send, pa_recv,
    pp_send, pp_recv, rs_send, rs_recv,
):
    tok, width = tokens.shape
    half = tok // 2
    depth = n // 2
    node = lax.axis_index("node")
    partner = 1 - lax.axis_index("local")
    row, column = node // 2, node % 2
    place = row * (1 - column) + (n - 1 - row) * column

    def node_at(position):
        side = position // depth
        level = position * (1 - side) + (n - 1 - position) * side
        return 2 * level + side

    to = (node_at((place + 1) % n), node_at((place + n - 1) % n))

    loads = [
        pltpu.make_async_copy(src, dst, weight_sem.at[k])
        for k, (src, dst) in enumerate(((wg_hbm, wg), (wu_hbm, wu), (wd_hbm, wd)))
    ]
    keep = pltpu.make_async_copy(
        tokens, x.at[0, pl.ds(0, tok), pl.ds(0, width)], own_sem.at[0]
    )
    keep.start()

    barrier = pltpu.get_barrier_semaphore()
    for target in ({"node": to[0]}, {"node": to[1]}, {"local": partner}):
        pl.semaphore_signal(barrier, inc=1, device_id=target, device_id_type=MESH)
    table_lane = lax.broadcasted_iota(jnp.int32, (tok, LANES), 1)
    table = jnp.zeros((tok, LANES), jnp.float32)
    for choice in range(ids.shape[1]):
        chosen = table_lane == ids[:, pl.ds(choice, 1)]
        table += jnp.where(chosen, values[:, pl.ds(choice, 1)].astype(jnp.float32), 0.0)
    x[0, pl.ds(0, tok), pl.ds(width, LANES)] = table.astype(jnp.bfloat16)
    keep.wait()
    pl.semaphore_wait(barrier, 3)

    def rows_of(d):
        return pl.ds(d * half, half)

    def ag(step, d, src):
        return pltpu.make_async_remote_copy(
            src_ref=src, dst_ref=x.at[step, rows_of(d)],
            send_sem=ag_send.at[step, d], recv_sem=ag_recv.at[step, d],
            device_id={"node": to[d]}, device_id_type=MESH,
        )

    def pa(step, src):
        return pltpu.make_async_remote_copy(
            src_ref=src, dst_ref=x.at[step, pl.ds(tok, tok)],
            send_sem=pa_send.at[step], recv_sem=pa_recv.at[step],
            device_id={"local": partner}, device_id_type=MESH,
        )

    def pp(step, slot):
        return pltpu.make_async_remote_copy(
            src_ref=pout.at[slot], dst_ref=pin.at[step],
            send_sem=pp_send.at[slot], recv_sem=pp_recv.at[step],
            device_id={"local": partner}, device_id_type=MESH,
        )

    def rs(i, d, slot):
        return pltpu.make_async_remote_copy(
            src_ref=acc.at[slot, rows_of(d)], dst_ref=ring_in.at[i - 1, rows_of(d)],
            send_sem=rs_send.at[slot, d], recv_sem=rs_recv.at[i - 1, d],
            device_id={"node": to[d]}, device_id_type=MESH,
        )

    for d in range(2):
        ag(1, d, x.at[0, rows_of(d)]).start()
    for load in loads:
        load.start()
    pa(0, x.at[0, pl.ds(0, tok)]).start()

    kc = chunk_of(width)

    def compute(step, slot):
        gate_acc[...] = jnp.zeros_like(gate_acc)
        up_acc[...] = jnp.zeros_like(up_acc)

        @pl.loop(0, width // kc)
        def _(k):
            cols = pl.ds(pl.multiple_of(k * kc, LANES), kc)
            rows = x[step, :, cols]
            gate_acc[...] += jnp.dot(rows, wg[cols, :], preferred_element_type=jnp.float32)
            up_acc[...] += jnp.dot(rows, wu[cols, :], preferred_element_type=jnp.float32)

        gate = gate_acc[...]
        hidden = (gate / (1.0 + jnp.exp(-gate)) * up_acc[...]).astype(jnp.bfloat16)
        table = x[step, :, pl.ds(width, LANES)].astype(jnp.float32)
        lane = lax.broadcasted_iota(jnp.int32, table.shape, 1)
        scale = jnp.sum(jnp.where(lane == node, table, 0.0), axis=1, keepdims=True)

        @pl.loop(0, width // kc)
        def _(k):
            cols = pl.ds(pl.multiple_of(k * kc, LANES), kc)
            value = jnp.dot(hidden, wd[:, cols], preferred_element_type=jnp.float32) * scale
            own[:, cols] = value[:tok]
            pout[slot, :, cols] = value[tok:].astype(jnp.bfloat16)

    def combine(step, i, d, dst, first):
        @pl.loop(0, width // kc)
        def _(k):
            cols = pl.ds(pl.multiple_of(k * kc, LANES), kc)
            value = own[rows_of(d), cols] + pin[step, rows_of(d), cols].astype(jnp.float32)
            if not first:
                value += ring_in[i - 2, rows_of(d), cols].astype(jnp.float32)
            dst[rows_of(d), cols] = value.astype(jnp.bfloat16)

    def gather_step(i, forward):
        for d in range(2):
            ag(i, d, x.at[0, rows_of(d)]).wait_recv()
            if forward:
                ag(i + 1, d, x.at[i, rows_of(d)]).start()
        pa(i, x.at[i, pl.ds(0, tok)]).start()

    def compute_step(i):
        pa(i, x.at[i, pl.ds(0, tok)]).wait_recv()
        compute(i, i % 2)
        pp(i, i % 2).start()

    def reduce_step(i, first):
        slot = i % 2
        pp(i, slot).wait_recv()
        for d in range(2):
            if not first:
                rs(i - 1, d, slot).wait_recv()
            combine(i, i, d, acc.at[slot], first)
            rs(i, d, slot).start()

    def free_slot(i):
        slot = i % 2

        @pl.when(i >= 3)
        def _():
            pp(i, slot).wait_send()
            for d in range(2):
                rs(i, d, slot).wait_send()

    gather_step(1, True)
    for load in loads:
        load.wait()
    compute_step(1)
    gather_step(2, True)
    reduce_step(1, True)

    @pl.loop(2, n - 2)
    def _(i):
        free_slot(i)
        compute_step(i)
        gather_step(i + 1, True)
        reduce_step(i, False)

    free_slot(n - 2)
    compute_step(n - 2)
    gather_step(n - 1, False)
    reduce_step(n - 2, False)
    free_slot(n - 1)
    compute_step(n - 1)
    reduce_step(n - 1, False)

    last = n % 2
    pa(0, x.at[0, pl.ds(0, tok)]).wait_recv()
    pp(0, last).wait_send()
    compute(0, last)
    pp(0, last).start()
    pp(0, last).wait_recv()
    for d in range(2):
        rs(n - 1, d, last).wait_recv()
        combine(0, n, d, out, False)
    for d in range(2):
        for slot in range(2):
            rs(1, d, slot).wait_send()

        @pl.loop(1, n)
        def _(i):
            ag(i, d, x.at[0, rows_of(d)]).wait_send()

    for slot in range(2):
        pp(0, slot).wait_send()

    @pl.loop(0, n)
    def _(i):
        pa(i, x.at[0, pl.ds(0, tok)]).wait_send()


def by_ring(n, tokens, gate_ids, gate_values, w_gate, w_up, w_down):
    tok, width = tokens.shape
    hid = w_gate.shape[2]
    half_type = jnp.bfloat16
    anywhere = pl.BlockSpec(memory_space=pl.ANY)
    in_vmem = pl.BlockSpec(memory_space=pltpu.VMEM)
    dma = pltpu.SemaphoreType.DMA
    return pl.pallas_call(
        functools.partial(ring_kernel, n),
        out_shape=jax.ShapeDtypeStruct((tok, width), half_type),
        in_specs=[anywhere, in_vmem, in_vmem, anywhere, anywhere, anywhere],
        out_specs=pl.BlockSpec(memory_space=pltpu.VMEM),
        scratch_shapes=[
            pltpu.VMEM((n, 2 * tok, width + LANES), half_type),
            pltpu.VMEM((width, hid), half_type),
            pltpu.VMEM((width, hid), half_type),
            pltpu.VMEM((hid, width), half_type),
            pltpu.VMEM((n - 1, tok, width), half_type),
            pltpu.VMEM((n, tok, width), half_type),
            pltpu.VMEM((2, tok, width), half_type),
            pltpu.VMEM((2, tok, width), half_type),
            pltpu.VMEM((tok, width), jnp.float32),
            pltpu.VMEM((2 * tok, hid), jnp.float32),
            pltpu.VMEM((2 * tok, hid), jnp.float32),
            dma((3,)), dma((1,)), dma((n, 2)), dma((n, 2)), dma((n,)), dma((n,)),
            dma((2,)), dma((n,)), dma((2, 2)), dma((n - 1, 2)),
        ],
        compiler_params=pltpu.CompilerParams(
            collective_id=0, has_side_effects=True, vmem_limit_bytes=VMEM_LIMIT
        ),
    )(tokens, gate_ids, gate_values, w_gate[0], w_up[0], w_down[0])


def by_collectives(tokens, gate_ids, gate_values, w_gate, w_up, w_down):
    n = lax.axis_size("node")
    every = ("node", "local")
    weights = lax.all_gather(expert_weights(gate_ids, gate_values, n), every, axis=0, tiled=True)
    rows = lax.all_gather(tokens, every, axis=0, tiled=True)
    mine = (jnp.arange(n, dtype=jnp.int32) == lax.axis_index("node"))[None, :]
    scale = jnp.sum(jnp.where(mine, weights.astype(jnp.float32), 0.0), axis=1, keepdims=True)
    gate_act = jnp.dot(rows, w_gate[0], preferred_element_type=jnp.float32)
    up_act = jnp.dot(rows, w_up[0], preferred_element_type=jnp.float32)
    hidden = (jax.nn.silu(gate_act) * up_act).astype(jnp.bfloat16)
    partial_value = jnp.dot(hidden, w_down[0], preferred_element_type=jnp.float32) * scale
    return lax.psum_scatter(
        partial_value.astype(jnp.bfloat16), every, scatter_dimension=0, tiled=True
    )


def ring_fits(n, tok, width, hid):
    rows = n * 2 * tok + (n - 1) * tok + n * tok + 7 * tok
    return 2 * width * (rows + 3 * hid) + 8 * 2 * tok * hid + 2**21 < VMEM_LIMIT


def per_device(tokens, gate_ids, gate_values, w_gate, w_up, w_down):
    n = lax.axis_size("node")
    fits = ring_fits(n, tokens.shape[0], tokens.shape[1], w_gate.shape[2])
    if n % 2 == 0 and n >= 4 and lax.axis_size("local") == 2 and n <= LANES and fits:
        return by_ring(n, tokens, gate_ids, gate_values, w_gate, w_up, w_down)
    return by_collectives(tokens, gate_ids, gate_values, w_gate, w_up, w_down)


def solution(mesh):
    return jax.shard_map(
        per_device,
        mesh=mesh,
        in_specs=(
            P(("rep", "node", "local"), None),
            P(("rep", "node", "local"), None),
            P(("rep", "node", "local"), None),
            P("node", None, "local"),
            P("node", None, "local"),
            P("node", "local", None),
        ),
        out_specs=P(("rep", "node", "local"), None),
        check_vma=False,
    )
```

```python
import functools

import jax
import jax.numpy as jnp
from jax import lax
from jax.experimental import pallas as pl
from jax.experimental.pallas import tpu as pltpu
from jax.sharding import PartitionSpec as P

MESH = pl.DeviceIdType.MESH
LANES = 128
PARTS = 4
ORDER = (0, 2, 1, 3)
VMEM_LIMIT = 67_000_000


def chunk_of(size, most=1024):
    chunk = most
    while size % chunk:
        chunk -= LANES
    return chunk


def expert_weights(gate_ids, gate_values, columns):
    expert_row = jnp.arange(columns, dtype=jnp.int32)
    return jnp.sum(
        jnp.where(
            gate_ids[:, :, None] == expert_row[None, None, :],
            gate_values.astype(jnp.float32)[:, :, None],
            jnp.float32(0.0),
        ),
        axis=1,
    ).astype(jnp.bfloat16)


def ring_kernel(
    n, tokens, ids, values, wg_hbm, wu_hbm, wd_hbm, out,
    x, wg, wu, wd, ring_in, pin, pout, acc, own, gate_acc, up_acc,
    weight_sem, own_sem, ag_send, ag_recv, pa_send, pa_recv,
    pp_send, pp_recv, rs_send, rs_recv,
):
    tok, width = tokens.shape
    part = tok // PARTS
    depth = n // 2
    node = lax.axis_index("node")
    partner = 1 - lax.axis_index("local")
    row, column = node // 2, node % 2
    place = row * (1 - column) + (n - 1 - row) * column

    def node_at(position):
        side = position // depth
        level = position * (1 - side) + (n - 1 - position) * side
        return 2 * level + side

    to = (node_at((place + 1) % n), node_at((place + n - 1) % n))

    loads = [
        pltpu.make_async_copy(src, dst, weight_sem.at[k])
        for k, (src, dst) in enumerate(((wg_hbm, wg), (wu_hbm, wu), (wd_hbm, wd)))
    ]
    keep = pltpu.make_async_copy(
        tokens, x.at[0, pl.ds(0, tok), pl.ds(0, width)], own_sem.at[0]
    )
    keep.start()

    barrier = pltpu.get_barrier_semaphore()
    for target in ({"node": to[0]}, {"node": to[1]}, {"local": partner}):
        pl.semaphore_signal(barrier, inc=1, device_id=target, device_id_type=MESH)
    table_row = lax.broadcasted_iota(jnp.int32, (LANES, tok), 0)
    turned = jnp.zeros((LANES, tok), jnp.float32)
    for choice in range(ids.shape[0]):
        chosen = table_row == ids[pl.ds(choice, 1), :]
        turned += jnp.where(chosen, values[pl.ds(choice, 1), :].astype(jnp.float32), 0.0)
    ones = lax.broadcasted_iota(jnp.int32, (tok, tok), 0) == lax.broadcasted_iota(
        jnp.int32, (tok, tok), 1
    )
    table = lax.dot_general(
        jnp.where(ones, 1.0, 0.0).astype(jnp.bfloat16), turned.astype(jnp.bfloat16),
        (((1,), (1,)), ((), ())), preferred_element_type=jnp.float32,
    )
    x[0, pl.ds(0, tok), pl.ds(width, LANES)] = table.astype(jnp.bfloat16)
    keep.wait()
    pl.semaphore_wait(barrier, 3)

    def rows_of(d):
        return pl.ds(d * part, part)

    def ag(step, d, src):
        return pltpu.make_async_remote_copy(
            src_ref=src, dst_ref=x.at[step, rows_of(d)],
            send_sem=ag_send.at[step, d], recv_sem=ag_recv.at[step, d],
            device_id={"node": to[d // 2]}, device_id_type=MESH,
        )

    def pa(step, src):
        return pltpu.make_async_remote_copy(
            src_ref=src, dst_ref=x.at[step, pl.ds(tok, tok)],
            send_sem=pa_send.at[step], recv_sem=pa_recv.at[step],
            device_id={"local": partner}, device_id_type=MESH,
        )

    def pp(step, slot):
        return pltpu.make_async_remote_copy(
            src_ref=pout.at[slot], dst_ref=pin.at[step],
            send_sem=pp_send.at[slot], recv_sem=pp_recv.at[step],
            device_id={"local": partner}, device_id_type=MESH,
        )

    def rs(i, d, slot):
        return pltpu.make_async_remote_copy(
            src_ref=acc.at[slot, rows_of(d)], dst_ref=ring_in.at[i - 1, rows_of(d)],
            send_sem=rs_send.at[slot, d], recv_sem=rs_recv.at[i - 1, d],
            device_id={"node": to[d // 2]}, device_id_type=MESH,
        )

    for d in ORDER:
        ag(1, d, x.at[0, rows_of(d)]).start()
    for load in loads:
        load.start()
    pa(0, x.at[0, pl.ds(0, tok)]).start()

    kc = chunk_of(width)

    def compute(step, slot):
        gate_acc[...] = jnp.zeros_like(gate_acc)
        up_acc[...] = jnp.zeros_like(up_acc)

        @pl.loop(0, width // kc)
        def _(k):
            cols = pl.ds(pl.multiple_of(k * kc, LANES), kc)
            rows = x[step, :, cols]
            gate_acc[...] += jnp.dot(rows, wg[cols, :], preferred_element_type=jnp.float32)
            up_acc[...] += jnp.dot(rows, wu[cols, :], preferred_element_type=jnp.float32)

        gate = gate_acc[...]
        hidden = (gate / (1.0 + jnp.exp(-gate)) * up_acc[...]).astype(jnp.bfloat16)
        table = x[step, :, pl.ds(width, LANES)].astype(jnp.float32)
        lane = lax.broadcasted_iota(jnp.int32, table.shape, 1)
        scale = jnp.sum(jnp.where(lane == node, table, 0.0), axis=1, keepdims=True)

        @pl.loop(0, width // kc)
        def _(k):
            cols = pl.ds(pl.multiple_of(k * kc, LANES), kc)
            value = jnp.dot(hidden, wd[:, cols], preferred_element_type=jnp.float32) * scale
            own[:, cols] = value[:tok]
            pout[slot, :, cols] = value[tok:].astype(jnp.bfloat16)

    def combine(step, i, d, dst, first):
        @pl.loop(0, width // kc)
        def _(k):
            cols = pl.ds(pl.multiple_of(k * kc, LANES), kc)
            value = own[rows_of(d), cols] + pin[step, rows_of(d), cols].astype(jnp.float32)
            if not first:
                value += ring_in[i - 2, rows_of(d), cols].astype(jnp.float32)
            dst[rows_of(d), cols] = value.astype(jnp.bfloat16)

    def gather_step(i, forward):
        for d in ORDER:
            ag(i, d, x.at[0, rows_of(d)]).wait_recv()
            if forward:
                ag(i + 1, d, x.at[i, rows_of(d)]).start()
        pa(i, x.at[i, pl.ds(0, tok)]).start()

    def compute_step(i):
        pa(i, x.at[i, pl.ds(0, tok)]).wait_recv()
        compute(i, i % 2)
        pp(i, i % 2).start()

    def reduce_step(i, first):
        slot = i % 2
        pp(i, slot).wait_recv()
        for d in ORDER:
            if not first:
                rs(i - 1, d, slot).wait_recv()
            combine(i, i, d, acc.at[slot], first)
            rs(i, d, slot).start()

    def free_slot(i):
        slot = i % 2

        @pl.when(i >= 3)
        def _():
            pp(i, slot).wait_send()
            for d in ORDER:
                rs(i, d, slot).wait_send()

    gather_step(1, True)
    for load in loads:
        load.wait()
    compute_step(1)
    gather_step(2, True)
    reduce_step(1, True)

    @pl.loop(2, n - 2)
    def _(i):
        free_slot(i)
        compute_step(i)
        gather_step(i + 1, True)
        reduce_step(i, False)

    free_slot(n - 2)
    compute_step(n - 2)
    gather_step(n - 1, False)
    reduce_step(n - 2, False)
    free_slot(n - 1)
    compute_step(n - 1)
    reduce_step(n - 1, False)

    last = n % 2
    pa(0, x.at[0, pl.ds(0, tok)]).wait_recv()
    pp(0, last).wait_send()
    compute(0, last)
    pp(0, last).start()
    pp(0, last).wait_recv()
    for d in ORDER:
        rs(n - 1, d, last).wait_recv()
        combine(0, n, d, out, False)
    for d in ORDER:
        for slot in range(2):
            rs(1, d, slot).wait_send()

        @pl.loop(1, n)
        def _(i):
            ag(i, d, x.at[0, rows_of(d)]).wait_send()

    for slot in range(2):
        pp(0, slot).wait_send()

    @pl.loop(0, n)
    def _(i):
        pa(i, x.at[0, pl.ds(0, tok)]).wait_send()


def by_ring(n, tokens, gate_ids, gate_values, w_gate, w_up, w_down):
    tok, width = tokens.shape
    hid = w_gate.shape[2]
    half_type = jnp.bfloat16
    anywhere = pl.BlockSpec(memory_space=pl.ANY)
    in_vmem = pl.BlockSpec(memory_space=pltpu.VMEM)
    dma = pltpu.SemaphoreType.DMA
    return pl.pallas_call(
        functools.partial(ring_kernel, n),
        out_shape=jax.ShapeDtypeStruct((tok, width), half_type),
        in_specs=[anywhere, in_vmem, in_vmem, anywhere, anywhere, anywhere],
        out_specs=pl.BlockSpec(memory_space=pltpu.VMEM),
        scratch_shapes=[
            pltpu.VMEM((n, 2 * tok, width + LANES), half_type),
            pltpu.VMEM((width, hid), half_type),
            pltpu.VMEM((width, hid), half_type),
            pltpu.VMEM((hid, width), half_type),
            pltpu.VMEM((n - 1, tok, width), half_type),
            pltpu.VMEM((n, tok, width), half_type),
            pltpu.VMEM((2, tok, width), half_type),
            pltpu.VMEM((2, tok, width), half_type),
            pltpu.VMEM((tok, width), jnp.float32),
            pltpu.VMEM((2 * tok, hid), jnp.float32),
            pltpu.VMEM((2 * tok, hid), jnp.float32),
            dma((3,)), dma((1,)), dma((n, PARTS)), dma((n, PARTS)), dma((n,)), dma((n,)),
            dma((2,)), dma((n,)), dma((2, PARTS)), dma((n - 1, PARTS)),
        ],
        compiler_params=pltpu.CompilerParams(
            collective_id=0, has_side_effects=True, vmem_limit_bytes=VMEM_LIMIT
        ),
    )(tokens, gate_ids.T, gate_values.T, w_gate[0], w_up[0], w_down[0])


def by_collectives(tokens, gate_ids, gate_values, w_gate, w_up, w_down):
    n = lax.axis_size("node")
    every = ("node", "local")
    weights = lax.all_gather(expert_weights(gate_ids, gate_values, n), every, axis=0, tiled=True)
    rows = lax.all_gather(tokens, every, axis=0, tiled=True)
    mine = (jnp.arange(n, dtype=jnp.int32) == lax.axis_index("node"))[None, :]
    scale = jnp.sum(jnp.where(mine, weights.astype(jnp.float32), 0.0), axis=1, keepdims=True)
    gate_act = jnp.dot(rows, w_gate[0], preferred_element_type=jnp.float32)
    up_act = jnp.dot(rows, w_up[0], preferred_element_type=jnp.float32)
    hidden = (jax.nn.silu(gate_act) * up_act).astype(jnp.bfloat16)
    partial_value = jnp.dot(hidden, w_down[0], preferred_element_type=jnp.float32) * scale
    return lax.psum_scatter(
        partial_value.astype(jnp.bfloat16), every, scatter_dimension=0, tiled=True
    )


def ring_fits(n, tok, width, hid):
    rows = n * 2 * tok + (n - 1) * tok + n * tok + 7 * tok
    return 2 * width * (rows + 3 * hid) + 8 * 2 * tok * hid + 2**21 < VMEM_LIMIT


def per_device(tokens, gate_ids, gate_values, w_gate, w_up, w_down):
    n = lax.axis_size("node")
    fits = ring_fits(n, tokens.shape[0], tokens.shape[1], w_gate.shape[2])
    if n % 2 == 0 and n >= 4 and tokens.shape[0] % 64 == 0 and lax.axis_size("local") == 2 and n <= LANES and fits:
        return by_ring(n, tokens, gate_ids, gate_values, w_gate, w_up, w_down)
    return by_collectives(tokens, gate_ids, gate_values, w_gate, w_up, w_down)


def solution(mesh):
    return jax.shard_map(
        per_device,
        mesh=mesh,
        in_specs=(
            P(("rep", "node", "local"), None),
            P(("rep", "node", "local"), None),
            P(("rep", "node", "local"), None),
            P("node", None, "local"),
            P("node", None, "local"),
            P("node", "local", None),
        ),
        out_specs=P(("rep", "node", "local"), None),
        check_vma=False,
    )
```
